32 devices in a mesh: seq: 8 (over y, x, core), head: 4 (over z).
Axes of the slice: x: 2, y: 2, z: 4, core: 2. Of those that a mesh axis runs over, the one named last changes fastest.
Arguments:
- tokens: bfloat16 [2048, 8192], P('seq', 'head'), may hold values from -12 to 12
- w_query: bfloat16 [8192, 4096], P(None, 'head'), may hold values from -0.100097656 to 0.100097656
- w_keyval: bfloat16 [8192, 512], P(None, 'head'), may hold values from -0.15039062 to 0.15039062
- w_out: bfloat16 [4096, 8192], P('head'), may hold values from -0.125 to 0.125
Outputs:
- layer_out: bfloat16 [2048, 8192], P('seq', 'head')
The draws below stay inside these ranges and needn't reach their ends.
All inputs are finite; a program needn't handle non-finite values.
Results may differ from the reference program's by a relative error of at most 0.0075.
The reference program's roundings to bfloat16 on the way (of `queries`, `keyval`, `product`, `weights` and `attended`) count: a program that leaves them out, or rounds other values in their place, can miss the bound.
Values may be sent and summed in bfloat16 or wider, within the bound.
A program may use at most 192 MiB of HBM per device.

```python
import math
import jax
import jax.numpy as jnp
from jax import lax

D = 8192
HEADS = 32
HEAD = 128
WIN1 = 512
WIN2 = 32
TOK_DEV = 256
TOKENS = 2048
HD = 4096


def draw_tokens(key, part):
    noise = jax.random.normal(jax.random.fold_in(key, 1), (TOKENS, D), jnp.float32)
    return jnp.clip(noise, -6.0, 6.0).astype(jnp.bfloat16)


def draw_w_query(key, part):
    values = jax.random.normal(jax.random.fold_in(key, 11), (D, HEADS * HEAD), jnp.float32) / math.sqrt(D)
    values = jnp.clip(values, -6.0 / math.sqrt(D), 6.0 / math.sqrt(D))
    return jnp.clip(values, -0.1, 0.1).astype(jnp.bfloat16)


def draw_w_keyval(key, part):
    values = 1.7 * jax.random.normal(jax.random.fold_in(key, 21), (D, 4 * HEAD), jnp.float32) / math.sqrt(D)
    values = jnp.clip(values, -10.2 / math.sqrt(D), 10.2 / math.sqrt(D))
    return jnp.clip(values, -0.15, 0.15).astype(jnp.bfloat16)


def with_spikes(result, own_key, source, target, parts, factor):
    owner, partner = [(jnp.arange(result.shape[dim]) // (result.shape[dim] // parts)).reshape([-1 if axis == dim else 1 for axis in range(result.ndim)]) for dim in (source, target)]
    chosen = jax.random.permutation(own_key, parts)[partner]
    strong = (owner == chosen) | (owner == (partner + parts // 2) % parts)
    return jnp.where(strong, factor * result, result)


def levels(key, shape, shards, low, largest):
    factor_of = 1.0
    for dim, parts in shards:
        draws = jax.random.uniform(jax.random.fold_in(jax.random.fold_in(key, 6), dim), (parts,), jnp.float32, low / len(shards), largest / len(shards))
        factor_of = factor_of * jnp.repeat(jnp.exp(draws), shape[dim] // parts).reshape((-1,) + (1,) * (len(shape) - 1 - dim))
    return factor_of


def gaussian_with(own_key, shape, spread, bound, split, heavy, kind=jnp.bfloat16):
    array = spread * jax.random.normal(own_key, shape, jnp.float32)
    if split:
        array = array * levels(own_key, shape, split, -0.22, 0.18)
    return jnp.clip(with_spikes(array, jax.random.fold_in(own_key, 3), *heavy), -bound, bound).astype(kind)


def setup_inputs(seed: int = 0) -> dict:
    seeds = jax.random.split(jax.random.key(seed), 5)
    tokens = draw_tokens(jax.random.fold_in(seeds[4], 71), 0)
    w_query = draw_w_query(jax.random.fold_in(seeds[4], 71), 0)
    w_keyval = draw_w_keyval(jax.random.fold_in(seeds[4], 71), 0)
    w_out = gaussian_with(seeds[3], (HD, D), HD ** -0.5, 0.125, ((0, 4),), (0, 1, 4, 2.0))
    return {"tokens": tokens, "w_query": w_query, "w_keyval": w_keyval, "w_out": w_out}


def window_rows(source, window, amount):
    return jnp.stack([source[window - 1 - lag_index: window - 1 - lag_index + amount] for lag_index in range(window)], axis=1)


def attend_block(query_rows, key_rows, value_rows, second_keys, second_values, first_pos):
    amount = query_rows.shape[0]
    window = second_keys.shape[0] - amount + 1
    lead = key_rows.shape[0] - amount
    key_two = window_rows(second_keys, window, amount)
    value_two = window_rows(second_values, window, amount)
    product = (query_rows.astype(jnp.float32)[:, None, :] * key_two.astype(jnp.float32)).astype(jnp.bfloat16)
    scores = jnp.einsum("ird,jd->irj", product.astype(jnp.float32), key_rows.astype(jnp.float32), precision=lax.Precision.HIGHEST) * (HEAD ** -0.5)
    row_ids = jnp.arange(amount, dtype=jnp.int32)[:, None, None]
    lag_ids = jnp.arange(window, dtype=jnp.int32)[None, :, None]
    column = jnp.arange(amount + lead, dtype=jnp.int32)[None, None, :]
    usable = (column >= row_ids) & (column <= row_ids + lead) & (first_pos - lead + column >= 0) & (first_pos + row_ids - lag_ids >= 0)
    row_peak = jnp.max(jnp.where(usable, scores, -jnp.inf), axis=(1, 2))
    raised = jnp.where(usable, jnp.exp(scores - row_peak[:, None, None]), 0.0)
    row_total = jnp.sum(raised, axis=(1, 2))
    weights = raised.astype(jnp.bfloat16)
    mixture = jnp.einsum("irj,jd->ird", weights.astype(jnp.float32), value_rows.astype(jnp.float32), precision=lax.Precision.HIGHEST)
    combined = jnp.sum(mixture * value_two.astype(jnp.float32), axis=1)
    return (combined / row_total[:, None]).astype(jnp.bfloat16)


def reference(tokens, w_query, w_keyval, w_out):
    queries = jnp.dot(tokens, w_query, preferred_element_type=jnp.float32).astype(jnp.bfloat16)
    keyval = jnp.dot(tokens, w_keyval, preferred_element_type=jnp.float32).astype(jnp.bfloat16)
    lead = WIN1 - 1
    first_pad = jnp.concatenate([jnp.zeros((lead, 2 * HEAD), jnp.bfloat16), keyval[:, :2 * HEAD]], axis=0)
    second_pad = jnp.concatenate([jnp.zeros((WIN2 - 1, 2 * HEAD), jnp.bfloat16), keyval[:, 2 * HEAD:]], axis=0)
    block = min(TOK_DEV, 128)
    block_count = TOKENS // block

    def one_block(block_index):
        offset = (block_index * block).astype(jnp.int32)
        first_rows = lax.dynamic_slice_in_dim(first_pad, offset, block + lead, 0)
        second_rows = lax.dynamic_slice_in_dim(second_pad, offset, block + WIN2 - 1, 0)

        def one_head(head_index):
            column_start = (head_index * HEAD).astype(jnp.int32)
            query_rows = lax.dynamic_slice(queries, (offset, column_start), (block, HEAD))
            return attend_block(query_rows, first_rows[:, :HEAD], first_rows[:, HEAD:], second_rows[:, :HEAD], second_rows[:, HEAD:], offset)

        return lax.map(one_head, jnp.arange(HEADS, dtype=jnp.int32))

    stacked = lax.map(one_block, jnp.arange(block_count, dtype=jnp.int32))
    attended = jnp.transpose(stacked, (0, 2, 1, 3)).reshape(TOKENS, HEADS * HEAD)
    return jnp.dot(attended, w_out, preferred_element_type=jnp.float32).astype(jnp.bfloat16)
```

```python
import functools

import jax
import jax.numpy as jnp
from jax import lax
from jax.experimental import pallas as pl
from jax.experimental.pallas import tpu as pltpu
from jax.sharding import PartitionSpec as P

HEAD = 128
WIN1 = 512
WIN2 = 32
GROUP = 16
BLOCK = 128
SHARES = (6, 6, 4)


def passed_along(value, axis, steps):
    count = lax.axis_size(axis)
    leading, last = (max(0, -steps), min(count, count - steps))
    return lax.ppermute(value, axis, [(source, source + steps) for source in range(leading, last)])


def attend_kernel(start, unroll, q_ref, kt_ref, vx_ref, k2_ref, v2_ref, o_ref, k2s, v2s):
    heads = q_ref.shape[1] // HEAD
    scale = HEAD ** -0.5 * 1.4426950408889634
    spread = (WIN2, GROUP, BLOCK)
    flat = (WIN2 * GROUP, BLOCK)

    def group_step(g, _):
        base = pl.multiple_of(g * GROUP, GROUP)
        place = pl.multiple_of(base + start, GROUP)
        block = (base + start) // BLOCK
        low = pl.multiple_of(block * BLOCK, BLOCK)
        keys = pl.ds(low, WIN1 + BLOCK)
        k2w = k2_ref[pl.ds(place, WIN2 + GROUP), :]
        v2w = v2_ref[pl.ds(place, WIN2 + GROUP), :]
        for r in range(WIN2):
            k2s[r] = k2w[WIN2 - r : WIN2 - r + GROUP].astype(jnp.bfloat16)
            v2s[r] = v2w[WIN2 - r : WIN2 - r + GROUP]
        row = lax.broadcasted_iota(jnp.int32, (1, GROUP, BLOCK), 1) + (place - low)
        col = lax.broadcasted_iota(jnp.int32, (1, GROUP, BLOCK), 2)
        fresh = jnp.broadcast_to(col <= row, spread).reshape(flat)

        def one(h):
            cols = pl.ds(pl.multiple_of(h * HEAD, HEAD), HEAD)
            q = q_ref[pl.ds(base, GROUP), cols]
            p = (q[None] * k2s[...]).reshape(WIN2 * GROUP, HEAD)
            s = jnp.dot(p, kt_ref[:, keys], preferred_element_type=jnp.float32)
            edge = jnp.where(fresh, s[:, WIN1:], s[:, :BLOCK])
            tiles = [edge] + [s[:, i * BLOCK : (i + 1) * BLOCK] for i in range(1, WIN1 // BLOCK)]
            top = functools.reduce(jnp.maximum, tiles).reshape(spread).max(axis=0)
            peak = jnp.max(top, axis=1, keepdims=True)
            peak = jnp.broadcast_to(peak[None], spread).reshape(flat)
            w = [jnp.exp2((x - peak) * scale).astype(jnp.bfloat16) for x in tiles]
            zero = jnp.zeros_like(w[0])
            w = jnp.concatenate(
                [jnp.where(fresh, zero, w[0])] + w[1:] + [jnp.where(fresh, w[0], zero)], axis=1
            )
            mix = jnp.dot(w, vx_ref[keys, :], preferred_element_type=jnp.float32)
            both = jnp.sum(mix.reshape(WIN2, GROUP, 2 * HEAD) * v2s[...], axis=0)
            o_ref[pl.ds(base, GROUP), cols] = (both[:, :HEAD] / both[:, HEAD:]).astype(jnp.bfloat16)

        def head_step(h, _):
            for u in range(unroll):
                one(h * unroll + u)
            return 0

        lax.fori_loop(0, heads // unroll, head_step, 0)
        return 0

    lax.fori_loop(0, q_ref.shape[0] // GROUP, group_step, 0)


def attend(start, q, kt, vx, k2, v2):
    heads = q.shape[1] // HEAD
    unroll = 8 if heads % 8 == 0 else 1
    exps = heads * q.shape[0] * WIN2 * WIN1
    return pl.pallas_call(
        functools.partial(attend_kernel, start, unroll),
        out_shape=jax.ShapeDtypeStruct(q.shape, jnp.bfloat16),
        in_specs=[pl.BlockSpec(memory_space=pltpu.VMEM)] * 5,
        out_specs=pl.BlockSpec(memory_space=pltpu.VMEM),
        scratch_shapes=[
            pltpu.VMEM((WIN2, GROUP, HEAD), jnp.bfloat16),
            pltpu.VMEM((WIN2, GROUP, 2 * HEAD), jnp.float32),
        ],
        cost_estimate=pl.CostEstimate(
            flops=exps * 1024, bytes_accessed=2 << 20, transcendentals=exps
        ),
        name="attend",
    )(q, kt, vx, k2, v2)


def window_parts(first_pair, second_pair, near_pair, far_pairs, near_tail):
    tok_rows = first_pair.shape[0]
    seq_index = lax.axis_index("seq")
    first = jnp.concatenate(far_pairs[::-1] + [near_pair, first_pair], axis=0)
    ahead = first.shape[0] - tok_rows
    position = seq_index * tok_rows - ahead + jnp.arange(first.shape[0], dtype=jnp.int32)[:, None]
    origin = jnp.clip(ahead - seq_index * tok_rows, 0, ahead)
    origin_key = lax.dynamic_slice(first[:, :HEAD], (origin, 0), (1, HEAD))
    real = position >= 0
    kt = jnp.where(real, first[:, :HEAD], origin_key).T
    vx = jnp.concatenate(
        [
            jnp.where(real, first[:, HEAD:], jnp.zeros((), first.dtype)),
            jnp.broadcast_to(real.astype(first.dtype), (first.shape[0], HEAD)),
        ],
        axis=1,
    )
    cut = ahead - WIN1
    kt, vx = kt[:, cut:], vx[cut:]
    second = jnp.concatenate([near_tail, second_pair], axis=0).astype(jnp.float32)
    spot = seq_index * tok_rows - WIN2 + jnp.arange(second.shape[0], dtype=jnp.int32)[:, None]
    real = spot >= 0
    k2 = jnp.where(real, second[:, :HEAD], second[WIN2 : WIN2 + 1, :HEAD])
    v2 = jnp.concatenate(
        [
            jnp.where(real, second[:, HEAD:], 0.0),
            jnp.broadcast_to(real.astype(jnp.float32), (second.shape[0], HEAD)),
        ],
        axis=1,
    )
    return kt, vx, k2, v2


def body(tokens, w_query, w_keyval, w_out):
    tok_rows = tokens.shape[0]
    piece = lax.all_gather(tokens, "head", axis=1, tiled=True)
    keyval_sum = jnp.dot(piece, w_keyval, preferred_element_type=jnp.float32)
    keyval = lax.all_gather(keyval_sum.astype(jnp.bfloat16), "head", axis=1, tiled=True)
    queries = jnp.dot(piece, w_query, preferred_element_type=jnp.float32).astype(jnp.bfloat16)
    first_pair = keyval[:, : 2 * HEAD]
    second_pair = keyval[:, 2 * HEAD :]
    tail_pair = second_pair[tok_rows - WIN2 :]
    near_pair, near_tail = passed_along((first_pair, tail_pair), "seq", 1)
    reach = -(-WIN1 // tok_rows)
    far_pairs = [passed_along(first_pair, "seq", step) for step in range(2, reach + 1)]
    parts = window_parts(first_pair, second_pair, near_pair, far_pairs, near_tail)
    start = 0
    pieces = []
    for share in SHARES:
        rows = tok_rows * share // sum(SHARES)
        attended = attend(start, queries[start : start + rows], *parts)
        attended, queries = lax.optimization_barrier((attended, queries))
        terms = jnp.dot(attended, w_out, preferred_element_type=jnp.float32).astype(jnp.bfloat16)
        pieces.append(lax.psum_scatter(terms, "head", scatter_dimension=1, tiled=True))
        start += rows
    return jnp.concatenate(pieces, axis=0)


def solution(mesh):
    return jax.shard_map(
        body,
        mesh=mesh,
        in_specs=(P("seq", "head"), P(None, "head"), P(None, "head"), P("head", None)),
        out_specs=P("seq", "head"),
        check_vma=False,
    )
```

```python
import functools

import jax
import jax.numpy as jnp
from jax import lax
from jax.experimental import pallas as pl
from jax.experimental.pallas import tpu as pltpu
from jax.sharding import PartitionSpec as P

HEAD = 128
WIN1 = 512
WIN2 = 32
GROUP = 16
BLOCK = 128
CHUNKS = 4


def passed_along(value, axis, steps):
    count = lax.axis_size(axis)
    leading, last = (max(0, -steps), min(count, count - steps))
    return lax.ppermute(value, axis, [(source, source + steps) for source in range(leading, last)])


def attend_group(place, row_at, q_ref, kt_ref, vx_ref, k2_ref, v2_ref, o_ref, k2s, v2s, unroll):
    heads = q_ref.shape[1] // HEAD
    scale = HEAD ** -0.5 * 1.4426950408889634
    spread = (WIN2, GROUP, BLOCK)
    flat = (WIN2 * GROUP, BLOCK)
    low = pl.multiple_of((place // BLOCK) * BLOCK, BLOCK)
    keys = pl.ds(low, WIN1 + BLOCK)
    k2w = k2_ref[pl.ds(place, WIN2 + GROUP), :]
    v2w = v2_ref[pl.ds(place, WIN2 + GROUP), :]
    for r in range(WIN2):
        k2s[r] = k2w[WIN2 - r : WIN2 - r + GROUP].astype(jnp.bfloat16)
        v2s[r] = v2w[WIN2 - r : WIN2 - r + GROUP]
    row = lax.broadcasted_iota(jnp.int32, (1, GROUP, BLOCK), 1) + (place - low)
    col = lax.broadcasted_iota(jnp.int32, (1, GROUP, BLOCK), 2)
    fresh = jnp.broadcast_to(col <= row, spread).reshape(flat)

    def one(h):
        cols = pl.ds(pl.multiple_of(h * HEAD, HEAD), HEAD)
        q = q_ref[pl.ds(place, GROUP), cols]
        p = (q[None] * k2s[...]).reshape(WIN2 * GROUP, HEAD)
        s = jnp.dot(p, kt_ref[:, keys], preferred_element_type=jnp.float32)
        edge = jnp.where(fresh, s[:, WIN1:], s[:, :BLOCK])
        tiles = [edge] + [s[:, i * BLOCK : (i + 1) * BLOCK] for i in range(1, WIN1 // BLOCK)]
        top = functools.reduce(jnp.maximum, tiles).reshape(spread).max(axis=0)
        peak = jnp.max(top, axis=1, keepdims=True)
        peak = jnp.broadcast_to(peak[None], spread).reshape(flat)
        w = [jnp.exp2((x - peak) * scale).astype(jnp.bfloat16) for x in tiles]
        zero = jnp.zeros_like(w[0])
        w = jnp.concatenate(
            [jnp.where(fresh, zero, w[0])] + w[1:] + [jnp.where(fresh, w[0], zero)], axis=1
        )
        mix = jnp.dot(w, vx_ref[keys, :], preferred_element_type=jnp.float32)
        both = jnp.sum(mix.reshape(WIN2, GROUP, 2 * HEAD) * v2s[...], axis=0)
        o_ref[pl.ds(row_at, GROUP), cols] = (both[:, :HEAD] / both[:, HEAD:]).astype(jnp.bfloat16)

    def head_step(h, _):
        for u in range(unroll):
            one(h * unroll + u)
        return 0

    lax.fori_loop(0, heads // unroll, head_step, 0)


def layer_kernel(
    n, chunk, unroll, q_ref, kt_ref, vx_ref, k2_ref, v2_ref, w_hbm, out_ref,
    k2s, v2s, att, w_ref, held, landed, own, w_sem, send_sem, recv_sem,
):
    tok_rows = q_ref.shape[0]
    chunks = tok_rows // chunk
    width = out_ref.shape[1]
    seq_at = lax.axis_index("seq")
    me = lax.axis_index("head")
    weights = pltpu.make_async_copy(w_hbm, w_ref, w_sem)
    weights.start()
    barrier = pltpu.get_barrier_semaphore()
    for away in range(1, n):
        pl.semaphore_signal(
            barrier, inc=1, device_id=(seq_at, lax.rem(me + away, n)),
            device_id_type=pl.DeviceIdType.MESH,
        )
    pl.semaphore_wait(barrier, n - 1)

    def sent(c, away):
        rows = pl.ds(pl.multiple_of(c * chunk, chunk), chunk)
        return pltpu.make_async_remote_copy(
            src_ref=held.at[away - 1, rows],
            dst_ref=landed.at[away - 1, rows],
            send_sem=send_sem.at[c, away - 1],
            recv_sem=recv_sem.at[c, away - 1],
            device_id=(seq_at, lax.rem(me + away, n)),
            device_id_type=pl.DeviceIdType.MESH,
        )

    def chunk_step(c, _):
        begin = pl.multiple_of(c * chunk, chunk)
        rows = pl.ds(begin, chunk)

        def group_step(g, _):
            row_at = pl.multiple_of(g * GROUP, GROUP)
            place = pl.multiple_of(begin + row_at, GROUP)
            attend_group(
                place, row_at, q_ref, kt_ref, vx_ref, k2_ref, v2_ref, att, k2s, v2s, unroll
            )
            return 0

        lax.fori_loop(0, chunk // GROUP, group_step, 0)

        @pl.when(c == 0)
        def _():
            weights.wait()

        for away in list(range(1, n)) + [0]:
            left = pl.multiple_of(lax.rem(me + away, n) * width, BLOCK)
            terms = jnp.dot(
                att[...], w_ref[:, pl.ds(left, width)], preferred_element_type=jnp.float32
            )
            if away:
                held[away - 1, rows, :] = terms.astype(jnp.bfloat16)
                sent(c, away).start()
            else:
                own[rows, :] = terms
        return 0

    lax.fori_loop(0, chunks, chunk_step, 0)

    def finish(c, _):
        rows = pl.ds(pl.multiple_of(c * chunk, chunk), chunk)
        total = own[rows, :]
        for away in range(1, n):
            sent(c, away).wait()
            total = total + landed[away - 1, rows, :].astype(jnp.float32)
        out_ref[rows, :] = total.astype(jnp.bfloat16)
        return 0

    lax.fori_loop(0, chunks, finish, 0)


def layer(n, q, kt, vx, k2, v2, w_out):
    tok_rows = q.shape[0]
    heads = q.shape[1] // HEAD
    chunk = tok_rows // CHUNKS
    unroll = 8 if heads % 8 == 0 else 1
    width = w_out.shape[1] // n
    return pl.pallas_call(
        functools.partial(layer_kernel, n, chunk, unroll),
        out_shape=jax.ShapeDtypeStruct((tok_rows, width), jnp.bfloat16),
        in_specs=[pl.BlockSpec(memory_space=pltpu.VMEM)] * 5 + [pl.BlockSpec(memory_space=pl.ANY)],
        out_specs=pl.BlockSpec(memory_space=pltpu.VMEM),
        scratch_shapes=[
            pltpu.VMEM((WIN2, GROUP, HEAD), jnp.bfloat16),
            pltpu.VMEM((WIN2, GROUP, 2 * HEAD), jnp.float32),
            pltpu.VMEM((chunk, q.shape[1]), jnp.bfloat16),
            pltpu.VMEM(w_out.shape, jnp.bfloat16),
            pltpu.VMEM((n - 1, tok_rows, width), jnp.bfloat16),
            pltpu.VMEM((n - 1, tok_rows, width), jnp.bfloat16),
            pltpu.VMEM((tok_rows, width), jnp.float32),
            pltpu.SemaphoreType.DMA,
            pltpu.SemaphoreType.DMA((CHUNKS, n - 1)),
            pltpu.SemaphoreType.DMA((CHUNKS, n - 1)),
        ],
        compiler_params=pltpu.CompilerParams(
            collective_id=1, has_side_effects=True, vmem_limit_bytes=58 << 20
        ),
        name="layer",
    )(q, kt, vx, k2, v2, w_out)


def window_parts(first_pair, second_pair, near_pair, far_pairs, near_tail):
    tok_rows = first_pair.shape[0]
    seq_index = lax.axis_index("seq")
    first = jnp.concatenate(far_pairs[::-1] + [near_pair, first_pair], axis=0)
    ahead = first.shape[0] - tok_rows
    position = seq_index * tok_rows - ahead + jnp.arange(first.shape[0], dtype=jnp.int32)[:, None]
    origin = jnp.clip(ahead - seq_index * tok_rows, 0, ahead)
    origin_key = lax.dynamic_slice(first[:, :HEAD], (origin, 0), (1, HEAD))
    real = position >= 0
    kt = jnp.where(real, first[:, :HEAD], origin_key).T
    vx = jnp.concatenate(
        [
            jnp.where(real, first[:, HEAD:], jnp.zeros((), first.dtype)),
            jnp.broadcast_to(real.astype(first.dtype), (first.shape[0], HEAD)),
        ],
        axis=1,
    )
    cut = ahead - WIN1
    kt, vx = kt[:, cut:], vx[cut:]
    second = jnp.concatenate([near_tail, second_pair], axis=0).astype(jnp.float32)
    spot = seq_index * tok_rows - WIN2 + jnp.arange(second.shape[0], dtype=jnp.int32)[:, None]
    real = spot >= 0
    k2 = jnp.where(real, second[:, :HEAD], second[WIN2 : WIN2 + 1, :HEAD])
    v2 = jnp.concatenate(
        [
            jnp.where(real, second[:, HEAD:], 0.0),
            jnp.broadcast_to(real.astype(jnp.float32), (second.shape[0], HEAD)),
        ],
        axis=1,
    )
    return kt, vx, k2, v2


def body(tokens, w_query, w_keyval, w_out):
    tok_rows = tokens.shape[0]
    piece = lax.all_gather(tokens, "head", axis=1, tiled=True)
    keyval_sum = jnp.dot(piece, w_keyval, preferred_element_type=jnp.float32)
    keyval = lax.all_gather(keyval_sum.astype(jnp.bfloat16), "head", axis=1, tiled=True)
    queries = jnp.dot(piece, w_query, preferred_element_type=jnp.float32).astype(jnp.bfloat16)
    first_pair = keyval[:, : 2 * HEAD]
    second_pair = keyval[:, 2 * HEAD :]
    tail_pair = second_pair[tok_rows - WIN2 :]
    near_pair, near_tail = passed_along((first_pair, tail_pair), "seq", 1)
    reach = -(-WIN1 // tok_rows)
    far_pairs = [passed_along(first_pair, "seq", step) for step in range(2, reach + 1)]
    parts = window_parts(first_pair, second_pair, near_pair, far_pairs, near_tail)
    return layer(lax.axis_size("head"), queries, *parts, w_out)


def solution(mesh):
    return jax.shard_map(
        body,
        mesh=mesh,
        in_specs=(P("seq", "head"), P(None, "head"), P(None, "head"), P("head", None)),
        out_specs=P("seq", "head"),
        check_vma=False,
    )
```

```python
import functools

import jax
import jax.numpy as jnp
from jax import lax
from jax.experimental import pallas as pl
from jax.experimental.pallas import tpu as pltpu
from jax.sharding import PartitionSpec as P

HEAD = 128
WIN1 = 512
WIN2 = 32
GROUP = 16
BLOCK = 128
CHUNKS = 4


def attend_group(place, row_at, q_ref, kt_ref, vx_ref, k2_ref, v2_ref, o_ref, k2s, v2s, unroll):
    heads = q_ref.shape[1] // HEAD
    scale = HEAD ** -0.5 * 1.4426950408889634
    spread = (WIN2, GROUP, BLOCK)
    flat = (WIN2 * GROUP, BLOCK)
    low = pl.multiple_of((place // BLOCK) * BLOCK, BLOCK)
    keys = pl.ds(low, WIN1 + BLOCK)
    k2w = k2_ref[pl.ds(place, WIN2 + GROUP), :]
    v2w = v2_ref[pl.ds(place, WIN2 + GROUP), :]
    for r in range(WIN2):
        k2s[r] = k2w[WIN2 - r : WIN2 - r + GROUP].astype(jnp.bfloat16)
        v2s[r] = v2w[WIN2 - r : WIN2 - r + GROUP]
    row = lax.broadcasted_iota(jnp.int32, (1, GROUP, BLOCK), 1) + (place - low)
    col = lax.broadcasted_iota(jnp.int32, (1, GROUP, BLOCK), 2)
    fresh = jnp.broadcast_to(col <= row, spread).reshape(flat)

    def one(h):
        cols = pl.ds(pl.multiple_of(h * HEAD, HEAD), HEAD)
        q = q_ref[pl.ds(place, GROUP), cols]
        p = (q[None] * k2s[...]).reshape(WIN2 * GROUP, HEAD)
        s = jnp.dot(p, kt_ref[:, keys], preferred_element_type=jnp.float32)
        edge = jnp.where(fresh, s[:, WIN1:], s[:, :BLOCK])
        tiles = [edge] + [s[:, i * BLOCK : (i + 1) * BLOCK] for i in range(1, WIN1 // BLOCK)]
        top = functools.reduce(jnp.maximum, tiles).reshape(spread).max(axis=0)
        peak = jnp.max(top, axis=1, keepdims=True)
        peak = jnp.broadcast_to(peak[None], spread).reshape(flat)
        w = [jnp.exp2((x - peak) * scale).astype(jnp.bfloat16) for x in tiles]
        zero = jnp.zeros_like(w[0])
        w = jnp.concatenate(
            [jnp.where(fresh, zero, w[0])] + w[1:] + [jnp.where(fresh, w[0], zero)], axis=1
        )
        mix = jnp.dot(w, vx_ref[keys, :], preferred_element_type=jnp.float32)
        both = jnp.sum(mix.reshape(WIN2, GROUP, 2 * HEAD) * v2s[...], axis=0)
        o_ref[pl.ds(row_at, GROUP), cols] = (both[:, :HEAD] / both[:, HEAD:]).astype(jnp.bfloat16)

    def head_step(h, _):
        for u in range(unroll):
            one(h * unroll + u)
        return 0

    lax.fori_loop(0, heads // unroll, head_step, 0)


def layer_kernel(
    n, chunk, unroll, q_ref, kt_ref, vx_ref, k2_ref, v2_ref, w_hbm, out_ref,
    k2s, v2s, att, w_ref, held, landed, own, w_sem, send_sem, recv_sem,
):
    tok_rows = q_ref.shape[0]
    chunks = tok_rows // chunk
    width = out_ref.shape[1]
    seq_at = lax.axis_index("seq")
    me = lax.axis_index("head")
    weights = pltpu.make_async_copy(w_hbm, w_ref, w_sem)
    weights.start()
    barrier = pltpu.get_barrier_semaphore()
    for away in range(1, n):
        pl.semaphore_signal(
            barrier, inc=1, device_id=(seq_at, lax.rem(me + away, n)),
            device_id_type=pl.DeviceIdType.MESH,
        )
    pl.semaphore_wait(barrier, n - 1)

    def sent(c, away):
        rows = pl.ds(pl.multiple_of(c * chunk, chunk), chunk)
        return pltpu.make_async_remote_copy(
            src_ref=held.at[away - 1, rows],
            dst_ref=landed.at[away - 1, rows],
            send_sem=send_sem.at[c, away - 1],
            recv_sem=recv_sem.at[c, away - 1],
            device_id=(seq_at, lax.rem(me + away, n)),
            device_id_type=pl.DeviceIdType.MESH,
        )

    def chunk_step(c, _):
        begin = pl.multiple_of(c * chunk, chunk)
        rows = pl.ds(begin, chunk)

        def group_step(g, _):
            row_at = pl.multiple_of(g * GROUP, GROUP)
            place = pl.multiple_of(begin + row_at, GROUP)
            attend_group(
                place, row_at, q_ref, kt_ref, vx_ref, k2_ref, v2_ref, att, k2s, v2s, unroll
            )
            return 0

        lax.fori_loop(0, chunk // GROUP, group_step, 0)

        @pl.when(c == 0)
        def _():
            weights.wait()

        for away in list(range(1, n)) + [0]:
            left = pl.multiple_of(lax.rem(me + away, n) * width, BLOCK)
            terms = jnp.dot(
                att[...], w_ref[:, pl.ds(left, width)], preferred_element_type=jnp.float32
            )
            if away:
                held[away - 1, rows, :] = terms.astype(jnp.bfloat16)
                sent(c, away).start()
            else:
                own[rows, :] = terms
        return 0

    lax.fori_loop(0, chunks, chunk_step, 0)

    def finish(c, _):
        rows = pl.ds(pl.multiple_of(c * chunk, chunk), chunk)
        total = own[rows, :]
        for away in range(1, n):
            sent(c, away).wait()
            total = total + landed[away - 1, rows, :].astype(jnp.float32)
        out_ref[rows, :] = total.astype(jnp.bfloat16)
        return 0

    lax.fori_loop(0, chunks, finish, 0)


def layer(n, q, kt, vx, k2, v2, w_out):
    tok_rows = q.shape[0]
    heads = q.shape[1] // HEAD
    chunk = tok_rows // CHUNKS
    unroll = 8 if heads % 8 == 0 else 1
    width = w_out.shape[1] // n
    return pl.pallas_call(
        functools.partial(layer_kernel, n, chunk, unroll),
        out_shape=jax.ShapeDtypeStruct((tok_rows, width), jnp.bfloat16),
        in_specs=[pl.BlockSpec(memory_space=pltpu.VMEM)] * 5 + [pl.BlockSpec(memory_space=pl.ANY)],
        out_specs=pl.BlockSpec(memory_space=pltpu.VMEM),
        scratch_shapes=[
            pltpu.VMEM((WIN2, GROUP, HEAD), jnp.bfloat16),
            pltpu.VMEM((WIN2, GROUP, 2 * HEAD), jnp.float32),
            pltpu.VMEM((chunk, q.shape[1]), jnp.bfloat16),
            pltpu.VMEM(w_out.shape, jnp.bfloat16),
            pltpu.VMEM((n - 1, tok_rows, width), jnp.bfloat16),
            pltpu.VMEM((n - 1, tok_rows, width), jnp.bfloat16),
            pltpu.VMEM((tok_rows, width), jnp.float32),
            pltpu.SemaphoreType.DMA,
            pltpu.SemaphoreType.DMA((CHUNKS, n - 1)),
            pltpu.SemaphoreType.DMA((CHUNKS, n - 1)),
        ],
        compiler_params=pltpu.CompilerParams(
            collective_id=1, has_side_effects=True, vmem_limit_bytes=58 << 20
        ),
        name="layer",
    )(q, kt, vx, k2, v2, w_out)


def front_kernel(
    n, seqs, reach, x_ref, wkv_ref, wq_hbm, q_out, kv_out, far_out, tail_out,
    wq, got, total, kv_total, kv, far, tail,
    w_sem, right_sem, left_sem, got_sem, kv_send, kv_recv, seq_send, seq_recv,
):
    depth = x_ref.shape[1]
    rows = x_ref.shape[0]
    me = lax.axis_index("head")
    seq_at = lax.axis_index("seq")
    tile = min(256, total.shape[1])

    def weights(source):
        part = pl.ds(pl.multiple_of(source * depth, depth), depth)
        return pltpu.make_async_copy(wq_hbm.at[part], wq.at[part], w_sem.at[source])

    for away in range(n):
        weights(lax.rem(me + away, n)).start()

    def signal(seq_to, head_to):
        pl.semaphore_signal(
            barrier, inc=1, device_id=(seq_to, head_to), device_id_type=pl.DeviceIdType.MESH
        )

    barrier = pltpu.get_barrier_semaphore()
    for away in range(1, n):
        signal(seq_at, lax.rem(me + away, n))
    for step in range(1, reach + 1):
        signal(lax.rem(seq_at + step, seqs), me)
        signal(lax.rem(seq_at + seqs - step, seqs), me)
    pl.semaphore_wait(barrier, n - 1 + 2 * reach)

    def remote(src, dst, send, recv, seq_to, head_to):
        return pltpu.make_async_remote_copy(
            src_ref=src, dst_ref=dst, send_sem=send, recv_sem=recv,
            device_id=(seq_to, head_to), device_id_type=pl.DeviceIdType.MESH,
        )

    def rightward(src, source):
        return remote(src, got.at[source], right_sem.at[source], got_sem.at[source], seq_at, me + 1)

    def leftward(src, source):
        return remote(src, got.at[source], left_sem.at[source], got_sem.at[source], seq_at, me - 1)

    @pl.when(me < n - 1)
    def _():
        rightward(x_ref, me).start()

    @pl.when(me > 0)
    def _():
        leftward(x_ref, me).start()

    def part_of(source):
        return pl.ds(pl.multiple_of(source * depth, depth), depth)

    def add_queries(block, source, fresh=False):
        weights(source).wait()

        def step(t, _):
            cols = pl.ds(pl.multiple_of(t * tile, tile), tile)
            terms = jnp.dot(
                block[...], wq[part_of(source), cols], preferred_element_type=jnp.float32
            )
            total[:, cols] = terms if fresh else total[:, cols] + terms
            return 0

        lax.fori_loop(0, total.shape[1] // tile, step, 0)

    def add_keyval(block, source):
        kv_total[...] += jnp.dot(
            block[...], wkv_ref[part_of(source), :], preferred_element_type=jnp.float32
        )

    kv_total[...] = jnp.zeros_like(kv_total)
    add_queries(x_ref, me, fresh=True)
    add_keyval(x_ref, me)

    def take(source, ahead, onward):
        onward_copy = onward(got.at[source], source)
        onward_copy.wait_recv()

        @pl.when(ahead)
        def _():
            onward_copy.start()
        add_keyval(got.at[source], source)

    def arrive(d, _):
        @pl.when(me - d >= 0)
        def _():
            take(me - d, me < n - 1, rightward)

        @pl.when(me + d < n)
        def _():
            take(me + d, me > 0, leftward)

        @pl.when((me - d >= 0) & (d < n - 1))
        def _():
            add_queries(got.at[me - d], me - d)

        @pl.when((me + d < n) & (d < n - 1))
        def _():
            add_queries(got.at[me + d], me + d)
        return 0

    lax.fori_loop(1, n, arrive, 0)
    kv[me] = kv_total[...].astype(jnp.bfloat16)

    def kv_copy(away):
        return remote(
            kv.at[me], kv.at[me], kv_send.at[away - 1], kv_recv.at[away - 1],
            seq_at, lax.rem(me + away, n),
        )

    for away in range(1, n):
        kv_copy(away).start()

    @pl.when((me == 0) | (me == n - 1))
    def _():
        add_queries(got.at[n - 1 - me], n - 1 - me)

    for away in range(1, n):
        kv_copy(away).wait()

    half = n // 2
    near = [
        lambda step=step: remote(
            kv.at[pl.ds(0, half)], far.at[step - 1], seq_send.at[step], seq_recv.at[step],
            seq_at + step, me,
        )
        for step in range(1, reach + 1)
    ]

    def tail_copy():
        return remote(
            kv.at[pl.ds(half, half), pl.ds(rows - WIN2, WIN2)], tail, seq_send.at[0],
            seq_recv.at[0], seq_at + 1, me,
        )

    @pl.when(seq_at + 1 < seqs)
    def _():
        tail_copy().start()

    for step in range(1, reach + 1):
        @pl.when(seq_at + step < seqs)
        def _():
            near[step - 1]().start()

    q_out[...] = total[...].astype(jnp.bfloat16)
    kv_out[...] = kv[...]

    @pl.when(seq_at >= 1)
    def _():
        tail_copy().wait_recv()
        tail_out[...] = tail[...]

    @pl.when(seq_at < 1)
    def _():
        tail_out[...] = jnp.zeros_like(tail_out)

    for step in range(1, reach + 1):
        @pl.when(seq_at >= step)
        def _():
            near[step - 1]().wait_recv()
            far_out[step - 1] = far[step - 1]

        @pl.when(seq_at < step)
        def _():
            far_out[step - 1] = jnp.zeros(far.shape[1:], far.dtype)

    @pl.when(seq_at + 1 < seqs)
    def _():
        tail_copy().wait_send()

    for step in range(1, reach + 1):
        @pl.when(seq_at + step < seqs)
        def _():
            near[step - 1]().wait_send()

    @pl.when(me < n - 1)
    def _():
        rightward(x_ref, me).wait_send()

    @pl.when(me > 0)
    def _():
        leftward(x_ref, me).wait_send()

    def settle(d, _):
        @pl.when((me - d >= 0) & (me < n - 1))
        def _():
            rightward(got.at[me - d], me - d).wait_send()

        @pl.when((me + d < n) & (me > 0))
        def _():
            leftward(got.at[me + d], me + d).wait_send()
        return 0

    lax.fori_loop(1, n, settle, 0)


def front(n, seqs, reach, tokens, w_query, w_keyval):
    rows, depth = tokens.shape
    width = w_keyval.shape[1]
    half = n // 2
    vmem = pl.BlockSpec(memory_space=pltpu.VMEM)
    shape = lambda *dims: jax.ShapeDtypeStruct(dims, jnp.bfloat16)
    dma = pltpu.SemaphoreType.DMA
    return pl.pallas_call(
        functools.partial(front_kernel, n, seqs, reach),
        out_shape=(
            shape(rows, w_query.shape[1]),
            shape(n, rows, width),
            shape(reach, half, rows, width),
            shape(half, WIN2, width),
        ),
        in_specs=[vmem, vmem, pl.BlockSpec(memory_space=pl.ANY)],
        out_specs=(vmem,) * 4,
        scratch_shapes=[
            pltpu.VMEM(w_query.shape, jnp.bfloat16),
            pltpu.VMEM((n, rows, depth), jnp.bfloat16),
            pltpu.VMEM((rows, w_query.shape[1]), jnp.float32),
            pltpu.VMEM((rows, width), jnp.float32),
            pltpu.VMEM((n, rows, width), jnp.bfloat16),
            pltpu.VMEM((reach, half, rows, width), jnp.bfloat16),
            pltpu.VMEM((half, WIN2, width), jnp.bfloat16),
            dma((n,)), dma((n,)), dma((n,)), dma((n,)),
            dma((n - 1,)), dma((n - 1,)), dma((reach + 1,)), dma((reach + 1,)),
        ],
        compiler_params=pltpu.CompilerParams(
            collective_id=2, has_side_effects=True, vmem_limit_bytes=58 << 20
        ),
        name="front",
    )(tokens, w_keyval, w_query)


def window_parts(first_pair, second_pair, near_pair, far_pairs, near_tail):
    tok_rows = first_pair.shape[0]
    seq_index = lax.axis_index("seq")
    first = jnp.concatenate(far_pairs[::-1] + [near_pair, first_pair], axis=0)
    ahead = first.shape[0] - tok_rows
    position = seq_index * tok_rows - ahead + jnp.arange(first.shape[0], dtype=jnp.int32)[:, None]
    origin = jnp.clip(ahead - seq_index * tok_rows, 0, ahead)
    origin_key = lax.dynamic_slice(first[:, :HEAD], (origin, 0), (1, HEAD))
    real = position >= 0
    kt = jnp.where(real, first[:, :HEAD], origin_key).T
    vx = jnp.concatenate(
        [
            jnp.where(real, first[:, HEAD:], jnp.zeros((), first.dtype)),
            jnp.broadcast_to(real.astype(first.dtype), (first.shape[0], HEAD)),
        ],
        axis=1,
    )
    cut = ahead - WIN1
    kt, vx = kt[:, cut:], vx[cut:]
    second = jnp.concatenate([near_tail, second_pair], axis=0).astype(jnp.float32)
    spot = seq_index * tok_rows - WIN2 + jnp.arange(second.shape[0], dtype=jnp.int32)[:, None]
    real = spot >= 0
    k2 = jnp.where(real, second[:, :HEAD], second[WIN2 : WIN2 + 1, :HEAD])
    v2 = jnp.concatenate(
        [
            jnp.where(real, second[:, HEAD:], 0.0),
            jnp.broadcast_to(real.astype(jnp.float32), (second.shape[0], HEAD)),
        ],
        axis=1,
    )
    return kt, vx, k2, v2


def side_by_side(blocks):
    return jnp.concatenate([blocks[i] for i in range(blocks.shape[0])], axis=1)


def body(tokens, w_query, w_keyval, w_out):
    n = lax.axis_size("head")
    reach = -(-WIN1 // tokens.shape[0])
    queries, keyval, earlier, tail = front(
        n, lax.axis_size("seq"), reach, tokens, w_query, w_keyval
    )
    keyval = side_by_side(keyval)
    pairs = [side_by_side(earlier[step]) for step in range(reach)]
    parts = window_parts(
        keyval[:, : 2 * HEAD], keyval[:, 2 * HEAD :], pairs[0], pairs[1:], side_by_side(tail)
    )
    return layer(n, queries, *parts, w_out)


def solution(mesh):
    return jax.shard_map(
        body,
        mesh=mesh,
        in_specs=(P("seq", "head"), P(None, "head"), P(None, "head"), P("head", None)),
        out_specs=P("seq", "head"),
        check_vma=False,
    )
```

```python
import functools

import jax
import jax.numpy as jnp
from jax import lax
from jax.experimental import pallas as pl
from jax.experimental.pallas import tpu as pltpu
from jax.sharding import PartitionSpec as P

HEAD = 128
WIN1 = 512
WIN2 = 32
GROUP = 16
BLOCK = 128
CHUNKS = 4


def attend_group(place, row_at, q_ref, kt_ref, vx_ref, k2_ref, v2_ref, o_ref, k2s, v2s, unroll):
    heads = q_ref.shape[1] // HEAD
    scale = HEAD ** -0.5 * 1.4426950408889634
    spread = (WIN2, GROUP, BLOCK)
    flat = (WIN2 * GROUP, BLOCK)
    low = pl.multiple_of((place // BLOCK) * BLOCK, BLOCK)
    keys = pl.ds(low, WIN1 + BLOCK)
    k2w = k2_ref[pl.ds(place, WIN2 + GROUP), :]
    v2w = v2_ref[pl.ds(place, WIN2 + GROUP), :]
    for r in range(WIN2):
        k2s[r] = k2w[WIN2 - r : WIN2 - r + GROUP].astype(jnp.bfloat16)
        v2s[r] = v2w[WIN2 - r : WIN2 - r + GROUP]
    row = lax.broadcasted_iota(jnp.int32, (1, GROUP, BLOCK), 1) + (place - low)
    col = lax.broadcasted_iota(jnp.int32, (1, GROUP, BLOCK), 2)
    fresh = jnp.broadcast_to(col <= row, spread).reshape(flat)

    def one(h):
        cols = pl.ds(pl.multiple_of(h * HEAD, HEAD), HEAD)
        q = q_ref[pl.ds(place, GROUP), cols]
        p = (q[None] * k2s[...]).reshape(WIN2 * GROUP, HEAD)
        s = jnp.dot(p, kt_ref[:, keys], preferred_element_type=jnp.float32)
        edge = jnp.where(fresh, s[:, WIN1:], s[:, :BLOCK])
        tiles = [edge] + [s[:, i * BLOCK : (i + 1) * BLOCK] for i in range(1, WIN1 // BLOCK)]
        top = functools.reduce(jnp.maximum, tiles).reshape(spread).max(axis=0)
        peak = jnp.max(top, axis=1, keepdims=True)
        peak = jnp.broadcast_to(peak[None], spread).reshape(flat)
        w = [jnp.exp2((x - peak) * scale).astype(jnp.bfloat16) for x in tiles]
        zero = jnp.zeros_like(w[0])
        w = jnp.concatenate(
            [jnp.where(fresh, zero, w[0])] + w[1:] + [jnp.where(fresh, w[0], zero)], axis=1
        )
        mix = jnp.dot(w, vx_ref[keys, :], preferred_element_type=jnp.float32)
        both = jnp.sum(mix.reshape(WIN2, GROUP, 2 * HEAD) * v2s[...], axis=0)
        o_ref[pl.ds(row_at, GROUP), cols] = (both[:, :HEAD] / both[:, HEAD:]).astype(jnp.bfloat16)

    def head_step(h, _):
        for u in range(unroll):
            one(h * unroll + u)
        return 0

    lax.fori_loop(0, heads // unroll, head_step, 0)


def layer_kernel(
    n, chunk, unroll, q_ref, kt_ref, vx_ref, k2_ref, v2_ref, w_hbm, out_ref,
    k2s, v2s, att, w_ref, held, landed, own, w_sem, send_sem, recv_sem,
):
    tok_rows = q_ref.shape[0]
    edge = chunk // 2
    width = out_ref.shape[1]
    seq_at = lax.axis_index("seq")
    me = lax.axis_index("head")
    weights = pltpu.make_async_copy(w_hbm, w_ref, w_sem)
    weights.start()
    barrier = pltpu.get_barrier_semaphore()
    for away in range(1, n):
        pl.semaphore_signal(
            barrier, inc=1, device_id=(seq_at, lax.rem(me + away, n)),
            device_id_type=pl.DeviceIdType.MESH,
        )
    pl.semaphore_wait(barrier, n - 1)

    def sent(c, begin, size, away):
        rows = pl.ds(begin, size)
        return pltpu.make_async_remote_copy(
            src_ref=held.at[away - 1, rows],
            dst_ref=landed.at[away - 1, rows],
            send_sem=send_sem.at[c, away - 1],
            recv_sem=recv_sem.at[c, away - 1],
            device_id=(seq_at, lax.rem(me + away, n)),
            device_id_type=pl.DeviceIdType.MESH,
        )

    def chunk_step(c, begin, size):
        rows = pl.ds(begin, size)

        def group_step(g, _):
            row_at = pl.multiple_of(g * GROUP, GROUP)
            place = pl.multiple_of(begin + row_at, GROUP)
            attend_group(
                place, row_at, q_ref, kt_ref, vx_ref, k2_ref, v2_ref, att, k2s, v2s, unroll
            )
            return 0

        lax.fori_loop(0, size // GROUP, group_step, 0)

        if isinstance(c, int) and c == 0:
            weights.wait()

        for away in list(range(1, n)) + [0]:
            left = pl.multiple_of(lax.rem(me + away, n) * width, BLOCK)
            terms = jnp.dot(
                att[:size, :], w_ref[:, pl.ds(left, width)], preferred_element_type=jnp.float32
            )
            if away:
                held[away - 1, rows, :] = terms.astype(jnp.bfloat16)
                sent(c, begin, size, away).start()
            else:
                own[rows, :] = terms

    def finish(c, begin, size):
        rows = pl.ds(begin, size)
        total = own[rows, :]
        for away in range(1, n):
            sent(c, begin, size, away).wait()
            total = total + landed[away - 1, rows, :].astype(jnp.float32)
        out_ref[rows, :] = total.astype(jnp.bfloat16)

    for run in (chunk_step, finish):
        run(0, 0, edge)

        def middle(c, _):
            run(c, pl.multiple_of(c * chunk - edge, edge), chunk)
            return 0

        lax.fori_loop(1, CHUNKS, middle, 0)
        run(CHUNKS, tok_rows - edge, edge)


def layer(n, q, kt, vx, k2, v2, w_out):
    tok_rows = q.shape[0]
    heads = q.shape[1] // HEAD
    chunk = tok_rows // CHUNKS
    unroll = 8 if heads % 8 == 0 else 1
    width = w_out.shape[1] // n
    return pl.pallas_call(
        functools.partial(layer_kernel, n, chunk, unroll),
        out_shape=jax.ShapeDtypeStruct((tok_rows, width), jnp.bfloat16),
        in_specs=[pl.BlockSpec(memory_space=pltpu.VMEM)] * 5 + [pl.BlockSpec(memory_space=pl.ANY)],
        out_specs=pl.BlockSpec(memory_space=pltpu.VMEM),
        scratch_shapes=[
            pltpu.VMEM((WIN2, GROUP, HEAD), jnp.bfloat16),
            pltpu.VMEM((WIN2, GROUP, 2 * HEAD), jnp.float32),
            pltpu.VMEM((chunk, q.shape[1]), jnp.bfloat16),
            pltpu.VMEM(w_out.shape, jnp.bfloat16),
            pltpu.VMEM((n - 1, tok_rows, width), jnp.bfloat16),
            pltpu.VMEM((n - 1, tok_rows, width), jnp.bfloat16),
            pltpu.VMEM((tok_rows, width), jnp.float32),
            pltpu.SemaphoreType.DMA,
            pltpu.SemaphoreType.DMA((CHUNKS + 1, n - 1)),
            pltpu.SemaphoreType.DMA((CHUNKS + 1, n - 1)),
        ],
        compiler_params=pltpu.CompilerParams(
            collective_id=1, has_side_effects=True, vmem_limit_bytes=58 << 20
        ),
        name="layer",
    )(q, kt, vx, k2, v2, w_out)


def front_kernel(
    n, seqs, reach, x_ref, wkv_ref, wq_hbm, q_out, kv_out, far_out, tail_out,
    wq, got, total, kv_total, kv, far, tail,
    w_sem, right_sem, left_sem, got_sem, kv_send, kv_recv, seq_send, seq_recv,
):
    depth = x_ref.shape[1]
    rows = x_ref.shape[0]
    me = lax.axis_index("head")
    seq_at = lax.axis_index("seq")
    tile = min(256, total.shape[1])

    def weights(source):
        part = pl.ds(pl.multiple_of(source * depth, depth), depth)
        return pltpu.make_async_copy(wq_hbm.at[part], wq.at[part], w_sem.at[source])

    for away in range(n):
        weights(lax.rem(me + away, n)).start()

    def signal(seq_to, head_to):
        pl.semaphore_signal(
            barrier, inc=1, device_id=(seq_to, head_to), device_id_type=pl.DeviceIdType.MESH
        )

    barrier = pltpu.get_barrier_semaphore()
    for away in range(1, n):
        signal(seq_at, lax.rem(me + away, n))
    for step in range(1, reach + 1):
        signal(lax.rem(seq_at + step, seqs), me)
        signal(lax.rem(seq_at + seqs - step, seqs), me)
    pl.semaphore_wait(barrier, n - 1 + 2 * reach)

    def remote(src, dst, send, recv, seq_to, head_to):
        return pltpu.make_async_remote_copy(
            src_ref=src, dst_ref=dst, send_sem=send, recv_sem=recv,
            device_id=(seq_to, head_to), device_id_type=pl.DeviceIdType.MESH,
        )

    def rightward(src, source):
        return remote(src, got.at[source], right_sem.at[source], got_sem.at[source], seq_at, me + 1)

    def leftward(src, source):
        return remote(src, got.at[source], left_sem.at[source], got_sem.at[source], seq_at, me - 1)

    @pl.when(me < n - 1)
    def _():
        rightward(x_ref, me).start()

    @pl.when(me > 0)
    def _():
        leftward(x_ref, me).start()

    def part_of(source):
        return pl.ds(pl.multiple_of(source * depth, depth), depth)

    def add_queries(block, source, fresh=False):
        weights(source).wait()

        def step(t, _):
            cols = pl.ds(pl.multiple_of(t * tile, tile), tile)
            terms = jnp.dot(
                block[...], wq[part_of(source), cols], preferred_element_type=jnp.float32
            )
            total[:, cols] = terms if fresh else total[:, cols] + terms
            return 0

        lax.fori_loop(0, total.shape[1] // tile, step, 0)

    def add_keyval(block, source):
        kv_total[...] += jnp.dot(
            block[...], wkv_ref[part_of(source), :], preferred_element_type=jnp.float32
        )

    kv_total[...] = jnp.zeros_like(kv_total)
    add_queries(x_ref, me, fresh=True)
    add_keyval(x_ref, me)

    def take(source, ahead, onward):
        onward_copy = onward(got.at[source], source)
        onward_copy.wait_recv()

        @pl.when(ahead)
        def _():
            onward_copy.start()
        add_keyval(got.at[source], source)

    def arrive(d, _):
        @pl.when(me - d >= 0)
        def _():
            take(me - d, me < n - 1, rightward)

        @pl.when(me + d < n)
        def _():
            take(me + d, me > 0, leftward)

        @pl.when((me - d >= 0) & (d < n - 1))
        def _():
            add_queries(got.at[me - d], me - d)

        @pl.when((me + d < n) & (d < n - 1))
        def _():
            add_queries(got.at[me + d], me + d)
        return 0

    lax.fori_loop(1, n, arrive, 0)
    kv[me] = kv_total[...].astype(jnp.bfloat16)

    def kv_copy(away):
        return remote(
            kv.at[me], kv.at[me], kv_send.at[away - 1], kv_recv.at[away - 1],
            seq_at, lax.rem(me + away, n),
        )

    for away in range(1, n):
        kv_copy(away).start()

    @pl.when((me == 0) | (me == n - 1))
    def _():
        add_queries(got.at[n - 1 - me], n - 1 - me)

    for away in range(1, n):
        kv_copy(away).wait()

    half = n // 2
    near = [
        lambda step=step: remote(
            kv.at[pl.ds(0, half)], far.at[step - 1], seq_send.at[step], seq_recv.at[step],
            seq_at + step, me,
        )
        for step in range(1, reach + 1)
    ]

    def tail_copy():
        return remote(
            kv.at[pl.ds(half, half), pl.ds(rows - WIN2, WIN2)], tail, seq_send.at[0],
            seq_recv.at[0], seq_at + 1, me,
        )

    @pl.when(seq_at + 1 < seqs)
    def _():
        tail_copy().start()

    for step in range(1, reach + 1):
        @pl.when(seq_at + step < seqs)
        def _():
            near[step - 1]().start()

    q_out[...] = total[...].astype(jnp.bfloat16)
    kv_out[...] = kv[...]

    @pl.when(seq_at >= 1)
    def _():
        tail_copy().wait_recv()
        tail_out[...] = tail[...]

    @pl.when(seq_at < 1)
    def _():
        tail_out[...] = jnp.zeros_like(tail_out)

    for step in range(1, reach + 1):
        @pl.when(seq_at >= step)
        def _():
            near[step - 1]().wait_recv()
            far_out[step - 1] = far[step - 1]

        @pl.when(seq_at < step)
        def _():
            far_out[step - 1] = jnp.zeros(far.shape[1:], far.dtype)

    @pl.when(seq_at + 1 < seqs)
    def _():
        tail_copy().wait_send()

    for step in range(1, reach + 1):
        @pl.when(seq_at + step < seqs)
        def _():
            near[step - 1]().wait_send()

    @pl.when(me < n - 1)
    def _():
        rightward(x_ref, me).wait_send()

    @pl.when(me > 0)
    def _():
        leftward(x_ref, me).wait_send()

    def settle(d, _):
        @pl.when((me - d >= 0) & (me < n - 1))
        def _():
            rightward(got.at[me - d], me - d).wait_send()

        @pl.when((me + d < n) & (me > 0))
        def _():
            leftward(got.at[me + d], me + d).wait_send()
        return 0

    lax.fori_loop(1, n, settle, 0)


def front(n, seqs, reach, tokens, w_query, w_keyval):
    rows, depth = tokens.shape
    width = w_keyval.shape[1]
    half = n // 2
    vmem = pl.BlockSpec(memory_space=pltpu.VMEM)
    shape = lambda *dims: jax.ShapeDtypeStruct(dims, jnp.bfloat16)
    dma = pltpu.SemaphoreType.DMA
    return pl.pallas_call(
        functools.partial(front_kernel, n, seqs, reach),
        out_shape=(
            shape(rows, w_query.shape[1]),
            shape(n, rows, width),
            shape(reach, half, rows, width),
            shape(half, WIN2, width),
        ),
        in_specs=[vmem, vmem, pl.BlockSpec(memory_space=pl.ANY)],
        out_specs=(vmem,) * 4,
        scratch_shapes=[
            pltpu.VMEM(w_query.shape, jnp.bfloat16),
            pltpu.VMEM((n, rows, depth), jnp.bfloat16),
            pltpu.VMEM((rows, w_query.shape[1]), jnp.float32),
            pltpu.VMEM((rows, width), jnp.float32),
            pltpu.VMEM((n, rows, width), jnp.bfloat16),
            pltpu.VMEM((reach, half, rows, width), jnp.bfloat16),
            pltpu.VMEM((half, WIN2, width), jnp.bfloat16),
            dma((n,)), dma((n,)), dma((n,)), dma((n,)),
            dma((n - 1,)), dma((n - 1,)), dma((reach + 1,)), dma((reach + 1,)),
        ],
        compiler_params=pltpu.CompilerParams(
            collective_id=2, has_side_effects=True, vmem_limit_bytes=58 << 20
        ),
        name="front",
    )(tokens, w_keyval, w_query)


def window_parts(first_pair, second_pair, near_pair, far_pairs, near_tail):
    tok_rows = first_pair.shape[0]
    seq_index = lax.axis_index("seq")
    first = jnp.concatenate(far_pairs[::-1] + [near_pair, first_pair], axis=0)
    ahead = first.shape[0] - tok_rows
    position = seq_index * tok_rows - ahead + jnp.arange(first.shape[0], dtype=jnp.int32)[:, None]
    origin = jnp.clip(ahead - seq_index * tok_rows, 0, ahead)
    origin_key = lax.dynamic_slice(first[:, :HEAD], (origin, 0), (1, HEAD))
    real = position >= 0
    kt = jnp.where(real, first[:, :HEAD], origin_key).T
    vx = jnp.concatenate(
        [
            jnp.where(real, first[:, HEAD:], jnp.zeros((), first.dtype)),
            jnp.broadcast_to(real.astype(first.dtype), (first.shape[0], HEAD)),
        ],
        axis=1,
    )
    cut = ahead - WIN1
    kt, vx = kt[:, cut:], vx[cut:]
    second = jnp.concatenate([near_tail, second_pair], axis=0).astype(jnp.float32)
    spot = seq_index * tok_rows - WIN2 + jnp.arange(second.shape[0], dtype=jnp.int32)[:, None]
    real = spot >= 0
    k2 = jnp.where(real, second[:, :HEAD], second[WIN2 : WIN2 + 1, :HEAD])
    v2 = jnp.concatenate(
        [
            jnp.where(real, second[:, HEAD:], 0.0),
            jnp.broadcast_to(real.astype(jnp.float32), (second.shape[0], HEAD)),
        ],
        axis=1,
    )
    return kt, vx, k2, v2


def side_by_side(blocks):
    return jnp.concatenate([blocks[i] for i in range(blocks.shape[0])], axis=1)


def body(tokens, w_query, w_keyval, w_out):
    n = lax.axis_size("head")
    reach = -(-WIN1 // tokens.shape[0])
    queries, keyval, earlier, tail = front(
        n, lax.axis_size("seq"), reach, tokens, w_query, w_keyval
    )
    keyval = side_by_side(keyval)
    pairs = [side_by_side(earlier[step]) for step in range(reach)]
    parts = window_parts(
        keyval[:, : 2 * HEAD], keyval[:, 2 * HEAD :], pairs[0], pairs[1:], side_by_side(tail)
    )
    return layer(n, queries, *parts, w_out)


def solution(mesh):
    return jax.shard_map(
        body,
        mesh=mesh,
        in_specs=(P("seq", "head"), P(None, "head"), P(None, "head"), P("head", None)),
        out_specs=P("seq", "head"),
        check_vma=False,
    )
```
